32 devices in a mesh: dp: 8 (over y, x, core), mp: 4 (over z).
Axes of the slice: x: 2, y: 2, z: 4, core: 2. Of those that a mesh axis runs over, the one named last changes fastest.
Arguments:
- activations: bfloat16 [8192, 8192], P('dp'), may hold values from -18 to 18
- curvature: float32 [8192, 2048], P('dp', 'mp'), may hold values from 0.05 to 5
- basis: float32 [12, 16777216], P(None, ('dp', 'mp')), may hold values from -6 to 6
- krylov: float32 [16777216], P(('dp', 'mp')), may hold values from -38 to 38
Outputs:
- new_vector: float32 [16777216], P(('dp', 'mp'))
- hessenberg: float32 [13], replicated
The draws below stay inside these ranges and needn't reach their ends.
All inputs are finite; a program needn't handle non-finite values.
Results may differ from the reference program's by a relative error of at most 0.0058.
Values may be sent and summed in bfloat16 or wider, within the bound.
No kernel may reach another device: no remote copies, remote signals or barrier semaphores. Data moves between devices by JAX's collectives and lax.ppermute only.
A program may use at most 128 MiB of HBM per device.

```python
import math
import jax
import jax.numpy as jnp
from jax import lax

D = 8192
BASIS = 12
KV = 1024
PARAMS = 16777216
TOKENS = 8192


def basis_row_stack(key):
    return jax.random.truncated_normal(jax.random.fold_in(key, 7), -6.0, 6.0, (BASIS, PARAMS), jnp.float32)


def draw_basis(key, part):
    return basis_row_stack(key)


def draw_krylov(key, part):
    stored = basis_row_stack(key)
    mixing = jax.random.uniform(jax.random.fold_in(key, 8), (BASIS,), jnp.float32, 0.5, 1.5)
    polarity = jnp.where(jax.random.normal(jax.random.fold_in(key, 9), (BASIS,), jnp.float32) > 0.0, 1.0, -1.0)
    noise_part = jax.random.truncated_normal(jax.random.fold_in(key, 10), -6.0, 6.0, (PARAMS,), jnp.float32)
    return (jnp.dot(mixing * polarity, stored, precision=lax.Precision.HIGHEST) + 0.6 * noise_part) / 3.0


def draw_activations(key, part):
    feature_scale = jnp.exp(jax.random.uniform(jax.random.fold_in(key, 3), (D,), jnp.float32, math.log(0.3), math.log(3.0)))
    values = jax.random.truncated_normal(jax.random.fold_in(key, 4), -6.0, 6.0, (TOKENS, D), jnp.float32)
    return (values * feature_scale[None, :]).astype(jnp.bfloat16)


def shard_levels(stream_key, extent, pieces, smallest, largest):
    level = 1.0
    for dim, shards_of in pieces:
        heights = jax.random.uniform(jax.random.fold_in(jax.random.fold_in(stream_key, 6), dim), (shards_of,), jnp.float32, smallest / len(pieces), largest / len(pieces))
        level = level * jnp.repeat(jnp.exp(heights), extent[dim] // shards_of).reshape((-1,) + (1,) * (len(extent) - 1 - dim))
    return level


def setup_inputs(seed: int = 0) -> dict:
    seeds = jax.random.split(jax.random.key(seed), 5)
    activations = draw_activations(jax.random.fold_in(seeds[4], 71), 0)
    curvature = jnp.clip(jnp.exp(math.log(5.0) - 4.6051702 * jax.random.uniform(seeds[1], (TOKENS, 2 * KV), jnp.float32) ** shard_levels(seeds[1], (TOKENS, 2 * KV), ((0, 8), (1, 4)), -0.2, 0.2)), 0.05, 5.0)
    basis = draw_basis(jax.random.fold_in(seeds[4], 71), 0)
    krylov = draw_krylov(jax.random.fold_in(seeds[4], 71), 0)
    return dict(activations=activations, curvature=curvature, basis=basis, krylov=krylov)


def reference(activations, curvature, basis, krylov):
    low_vector = krylov.astype(jnp.bfloat16).reshape(D, 2 * KV)
    projected_coefficients = jnp.dot(activations, low_vector, preferred_element_type=jnp.float32)
    weighted = (curvature * projected_coefficients).astype(jnp.bfloat16)
    gradient = lax.dot_general(activations, weighted, (((0,), (0,)), ((), ())), preferred_element_type=jnp.float32)
    curved = (gradient / TOKENS).reshape(PARAMS)
    coeffs = jnp.dot(basis, curved, precision=lax.Precision.HIGHEST) / PARAMS
    residual_vector = curved - jnp.dot(coeffs, basis, precision=lax.Precision.HIGHEST)
    mean_square = jnp.sum(residual_vector * residual_vector) / PARAMS
    scale_norm = jnp.sqrt(mean_square + 1e-06)
    return (residual_vector / scale_norm, jnp.concatenate([coeffs, scale_norm[None]]))
```

```python
import functools

import jax
import jax.numpy as jnp
from jax import lax
from jax.experimental import pallas as pl
from jax.experimental.pallas import tpu as pltpu
from jax.sharding import PartitionSpec as P

LANES = 128
SUB = 8
TILES = 16
CHUNKS = 2
F32, BF16 = jnp.float32, jnp.bfloat16
VMEM = pl.BlockSpec(memory_space=pltpu.VMEM)
SMEM = pl.BlockSpec(memory_space=pltpu.SMEM)


def params(**kw):
    return pltpu.CompilerParams(vmem_limit_bytes=48 * 1024 * 1024, **kw)


def cost(flops, nbytes):
    return pl.CostEstimate(flops=int(flops), bytes_accessed=int(nbytes), transcendentals=0)


def pack_kernel(mp, rows, m_ref, x_ref, *outs):
    per = TILES // mp
    width = outs[0].shape[1] // LANES
    for s in range(mp):
        dest = lax.rem(m_ref[0] + s, mp)
        for t in range(per):
            part = x_ref[pl.ds(dest * per + t, rows, stride=TILES), :].astype(BF16)
            out = outs[(t // width) * mp + s]
            out[:, pl.ds((t % width) * LANES, LANES)] = part


def pack(m, krylov, mp, rows, cw, chunks):
    outs = pl.pallas_call(
        functools.partial(pack_kernel, mp, rows),
        out_shape=[jax.ShapeDtypeStruct((rows, cw), BF16)] * (mp * chunks),
        in_specs=[SMEM, VMEM],
        out_specs=[VMEM] * (mp * chunks),
        compiler_params=params(),
        cost_estimate=cost(0, krylov.size * 6),
        name="pack",
    )(m, krylov)
    return [outs[c * mp : (c + 1) * mp] for c in range(chunks)]


def assemble_kernel(mp, rows, m_ref, *refs):
    out = refs[-1]
    for s in range(mp):
        src = lax.rem(m_ref[0] + (mp - s), mp)
        out[pl.ds(pl.multiple_of(src * rows, rows), rows), :] = refs[s][...]


def assemble(m, pieces):
    mp = len(pieces)
    rows, cw = pieces[0].shape
    return pl.pallas_call(
        functools.partial(assemble_kernel, mp, rows),
        out_shape=jax.ShapeDtypeStruct((mp * rows, cw), BF16),
        in_specs=[SMEM] + [VMEM] * mp,
        out_specs=VMEM,
        compiler_params=params(),
        cost_estimate=cost(0, mp * rows * cw * 4),
        name="assemble",
    )(m, *pieces)


def matmul_kernel(n, groups, idx_ref, act_ref, curv_ref, *refs):
    blocks = refs[:n]
    outs = refs[n : n + len(groups)]
    acc, wt = refs[n + len(groups) :]
    step = pl.program_id(0)
    for k in range(n):

        @pl.when(step == k)
        def _(k=k):
            part = jnp.dot(act_ref[...], blocks[k][...], preferred_element_type=F32)
            if k == 0:
                acc[...] = part
            elif k < n - 1:
                acc[...] += part
            else:
                weighted = (acc[...] + part) * curv_ref[...]
                wt[...] = weighted.T.astype(BF16)

    for (first, count, dtype), out in zip(groups, outs):

        @pl.when((step >= n + first) & (step < n + first + count))
        def _(out=out, dtype=dtype):
            out[0] = jnp.dot(wt[...], act_ref[...], preferred_element_type=F32).astype(dtype)


def matmuls(idx, activations, curvature, blocks, chunk, groups):
    n = len(blocks)
    tok = activations.shape[0]
    rows, cw = blocks[0].shape
    out_specs = [
        pl.BlockSpec(
            (1, cw, rows),
            lambda t, i, first=first, count=count: (jnp.clip(t - n - first, 0, count - 1), 0, 0),
        )
        for first, count, _ in groups
    ]
    return pl.pallas_call(
        functools.partial(matmul_kernel, n, groups),
        out_shape=[jax.ShapeDtypeStruct((count, cw, rows), dt) for _, count, dt in groups],
        grid_spec=pltpu.PrefetchScalarGridSpec(
            num_scalar_prefetch=1,
            grid=(2 * n,),
            in_specs=[
                pl.BlockSpec((tok, rows), lambda t, i: (0, i[lax.rem(t, n)])),
                pl.BlockSpec((tok, cw), lambda t, i: (0, chunk), pipeline_mode=pl.Buffered(1)),
            ]
            + [pl.BlockSpec((rows, cw), lambda t, i: (0, 0), pipeline_mode=pl.Buffered(1))] * n,
            out_specs=out_specs,
            scratch_shapes=[pltpu.VMEM((tok, cw), F32), pltpu.VMEM((cw, tok), BF16)],
        ),
        compiler_params=params(dimension_semantics=("arbitrary",)),
        cost_estimate=cost(4 * tok * rows * n * cw, 4 * tok * rows * n),
        name="matmuls",
    )(idx, activations, curvature, *blocks)


def split_kernel(mp, rows, scale, m_ref, *refs):
    terms, outs, tmp = refs[: -mp - 1], refs[-mp - 1 : -1], refs[-1]
    total = terms[0][...].astype(F32)
    for t in terms[1:]:
        total += t[...].astype(F32)
    tmp[...] = (total * scale).T
    for s in range(mp):
        dest = lax.rem(m_ref[0] + s, mp)
        outs[s][...] = tmp[pl.ds(pl.multiple_of(dest * rows, rows), rows), :].astype(BF16)


def split(m, terms, mp, scale):
    cw, depth = terms[0].shape
    rows = depth // mp
    return pl.pallas_call(
        functools.partial(split_kernel, mp, rows, scale),
        out_shape=[jax.ShapeDtypeStruct((rows, cw), BF16)] * mp,
        in_specs=[SMEM] + [VMEM] * len(terms),
        out_specs=[VMEM] * mp,
        scratch_shapes=[pltpu.VMEM((depth, cw), F32)],
        compiler_params=params(),
        cost_estimate=cost(0, cw * depth * 12),
        name="split",
    )(m, *terms)


def rot(x, k):
    return x if k == 0 else pltpu.roll(x, SUB - k, 0)


def gram_kernel(basis_ref, out_ref):
    hi = basis_ref.shape[0] - SUB

    @pl.when(pl.program_id(0) == 0)
    def _():
        out_ref[...] = jnp.zeros_like(out_ref)

    half = lax.broadcasted_iota(jnp.int32, (SUB, LANES), 0) < hi

    def body(g, acc):
        at = pl.ds(pl.multiple_of(g * LANES, LANES), LANES)
        b0 = basis_ref[0:SUB, at]
        b1 = basis_ref[SUB : SUB + hi, at]
        b1 = jnp.concatenate([b1, b1], axis=0)
        new = [b0 * rot(b0, k) for k in range(5)]
        new += [b1 * rot(b1, k) for k in range(3)]
        new += [b0 * rot(b1, k) for k in range(4)]
        return tuple(a + v for a, v in zip(acc, new))

    count = basis_ref.shape[1] // LANES
    acc = lax.fori_loop(
        0, count, body, tuple(jnp.zeros((SUB, LANES), F32) for _ in range(12)), unroll=4
    )
    for k in range(12):
        out_ref[k] += acc[k]


def gram(basis, blocks):
    nb, length = basis.shape
    return pl.pallas_call(
        gram_kernel,
        out_shape=jax.ShapeDtypeStruct((12, SUB, LANES), F32),
        grid=(blocks,),
        in_specs=[pl.BlockSpec((nb, length // blocks), lambda t: (0, t))],
        out_specs=pl.BlockSpec((12, SUB, LANES), lambda t: (0, 0, 0)),
        compiler_params=params(dimension_semantics=("arbitrary",)),
        cost_estimate=cost(24 * SUB * length, basis.size * 4),
        name="gram",
    )(basis)


def project_kernel(mp, chunks, m_ref, gram_ref, basis_ref, *refs):
    pieces = refs[: mp * chunks]
    u_ref, sums_ref, acc = refs[mp * chunks :]
    nb = basis_ref.shape[0]
    step = pl.program_id(0)
    rows, cw = pieces[0].shape
    per = TILES // mp
    width = cw // LANES
    for s in range(mp):
        src = lax.rem(m_ref[0] + (mp - s), mp)
        for t in range(per):
            piece = pieces[(t // width) * mp + s]
            u_ref[pl.ds(src * per + t, rows, stride=TILES), :] = piece[
                :, pl.ds((t % width) * LANES, LANES)
            ].astype(F32)

    @pl.when(step == 0)
    def _():
        acc[...] = jnp.zeros_like(acc)

    def body(q, carry):
        c0, c1, sq = carry
        base = pl.multiple_of(q * SUB, SUB)
        u = u_ref[pl.ds(base, SUB), :]
        sq = sq + u * u
        for g in range(SUB):
            at = pl.ds(pl.multiple_of((base + g) * LANES, LANES), LANES)
            ug = jnp.broadcast_to(u[g : g + 1, :], (SUB, LANES))
            c0 = c0 + basis_ref[0:SUB, at] * ug
            c1 = c1 + basis_ref[SUB:nb, at] * ug[: nb - SUB]
        return c0, c1, sq

    zero = jnp.zeros((SUB, LANES), F32)
    c0, c1, sq = lax.fori_loop(
        0, rows * TILES // SUB, body, (zero, zero[: nb - SUB], zero), unroll=2
    )
    acc[0] += c0
    acc[1, 0 : nb - SUB] += c1
    acc[2] += sq

    @pl.when(step == pl.num_programs(0) - 1)
    def _():
        lane = lax.broadcasted_iota(jnp.int32, (SUB, LANES), 1)
        tile = jnp.zeros((SUB, LANES), F32)
        for k in range(15):
            part = gram_ref[k] if k < 12 else acc[k - 12]
            tile = jnp.where(lane == k, jnp.sum(part, axis=1, keepdims=True), tile)
        sums_ref[...] = jnp.broadcast_to(tile[None], sums_ref.shape)


def project(m, gram_tiles, basis, pieces, mp, devices, blocks):
    nb, length = basis.shape
    chunks = len(pieces)
    flat = [p for c in pieces for p in c]
    rows, cw = flat[0].shape
    return pl.pallas_call(
        functools.partial(project_kernel, mp, chunks),
        out_shape=[
            jax.ShapeDtypeStruct((length // LANES, LANES), F32),
            jax.ShapeDtypeStruct((devices, SUB, LANES), F32),
        ],
        grid=(blocks,),
        in_specs=[
            SMEM,
            pl.BlockSpec((12, SUB, LANES), lambda t: (0, 0, 0)),
            pl.BlockSpec((nb, length // blocks), lambda t: (0, t)),
        ]
        + [pl.BlockSpec((rows // blocks, cw), lambda t: (t, 0))] * len(flat),
        out_specs=[
            pl.BlockSpec((length // LANES // blocks, LANES), lambda t: (t, 0)),
            pl.BlockSpec((devices, SUB, LANES), lambda t: (0, 0, 0)),
        ],
        scratch_shapes=[pltpu.VMEM((3, SUB, LANES), F32)],
        compiler_params=params(dimension_semantics=("arbitrary",)),
        cost_estimate=cost(4 * SUB * length, basis.size * 4),
        name="project",
    )(m, gram_tiles, basis, *flat)


def residual_kernel(total, nb, sums_ref, basis_ref, u_ref, out_ref, hess_ref, held):
    @pl.when(pl.program_id(0) == 0)
    def _():
        tile = jnp.sum(sums_ref[...], axis=0) / total
        hi = nb - SUB
        col = lambda k: jnp.broadcast_to(tile[:, k : k + 1], (SUB, LANES))
        sub = lax.broadcasted_iota(jnp.int32, (SUB, LANES), 0)
        lane = lax.broadcasted_iota(jnp.int32, (SUB, LANES), 1)
        c0 = col(12)
        c1 = jnp.where(sub < hi, col(13), 0.0)
        twice = c1 + rot(c1, SUB - hi)
        quad = jnp.zeros((SUB, LANES), F32)
        for k in range(5):
            quad += (1.0 if k in (0, 4) else 2.0) * c0 * rot(c0, k) * col(k)
        for k in range(3):
            term = twice * rot(twice, k) * col(5 + k)
            quad += jnp.where(sub < hi, (1.0 if k in (0, 2) else 2.0) * term, 0.0)
        for k in range(4):
            quad += 2.0 * c0 * rot(twice, k) * col(8 + k)
        quad += col(14) - 2.0 * (c0 * c0 + c1 * c1)
        mean_square = jnp.maximum(jnp.sum(quad, axis=0, keepdims=True), 0.0)
        norm = jnp.broadcast_to(jnp.sqrt(mean_square + 1e-06), (SUB, LANES))
        held[0] = c0
        held[1] = c1
        held[2] = 1.0 / norm
        line = jnp.sum(jnp.where(sub == lane, c0, 0.0), axis=0, keepdims=True)
        line += jnp.sum(jnp.where(sub + SUB == lane, c1, 0.0), axis=0, keepdims=True)
        lane1 = lax.broadcasted_iota(jnp.int32, (1, LANES), 1)
        hess_ref[...] = jnp.where(lane1 == nb, norm[0:1], line)

    c0 = held[0]
    c1 = held[1][: nb - SUB]
    inv = held[2]

    def body(q, carry):
        base = pl.multiple_of(q * SUB, SUB)
        rows = []
        for g in range(SUB):
            at = pl.ds(pl.multiple_of((base + g) * LANES, LANES), LANES)
            t0 = jnp.sum(basis_ref[0:SUB, at] * c0, axis=0, keepdims=True)
            t1 = jnp.sum(basis_ref[SUB:nb, at] * c1, axis=0, keepdims=True)
            rows.append(t0 + t1)
        at = pl.ds(base, SUB)
        out_ref[at, :] = (u_ref[at, :] - jnp.concatenate(rows, axis=0)) * inv
        return carry

    lax.fori_loop(0, out_ref.shape[0] // SUB, body, 0, unroll=2)


def residual(sums, basis, u, total, blocks):
    nb, length = basis.shape
    return pl.pallas_call(
        functools.partial(residual_kernel, total, nb),
        out_shape=[
            jax.ShapeDtypeStruct((length // LANES, LANES), F32),
            jax.ShapeDtypeStruct((1, LANES), F32),
        ],
        grid=(blocks,),
        in_specs=[
            pl.BlockSpec(sums.shape, lambda t: (0, 0, 0)),
            pl.BlockSpec((nb, length // blocks), lambda t: (0, t)),
            pl.BlockSpec((length // LANES // blocks, LANES), lambda t: (t, 0)),
        ],
        out_specs=[
            pl.BlockSpec((length // LANES // blocks, LANES), lambda t: (t, 0)),
            pl.BlockSpec((1, LANES), lambda t: (0, 0)),
        ],
        scratch_shapes=[pltpu.VMEM((3, SUB, LANES), F32)],
        compiler_params=params(dimension_semantics=("arbitrary",)),
        cost_estimate=cost(4 * SUB * length, basis.size * 4),
        name="residual",
    )(sums, basis, u)


def shift_mp(pieces):
    mp = len(pieces)
    return [pieces[0]] + [
        lax.ppermute(pieces[s], "mp", [(i, (i + s) % mp) for i in range(mp)])
        for s in range(1, mp)
    ]


def partner(x):
    n = lax.axis_size("dp")
    return lax.ppermute(x, "dp", [(i, i ^ 1) for i in range(n)])


def along(x):
    n = lax.axis_size("dp")
    return lax.ppermute(x, "dp", [(i, i ^ (4 if i % 2 else 2)) for i in range(n)])


def cube_gather(own):
    beside = partner(own)
    one = along(own)
    two = along(beside)
    one_beside = partner(one)
    three = along(one_beside)
    two_beside = partner(two)
    return [own, one, two, three, beside, one_beside, two_beside, partner(three)]


def cube_order(d):
    a = jnp.where(d % 2 == 1, 4, 2)
    b = 6 - a
    rel = [d * 0, a, a ^ 1, a ^ b ^ 1, d * 0 + 1, b ^ 1, b, a ^ b]
    return jnp.stack([d ^ r for r in rel]).astype(jnp.int32)


CUBE_GROUPS = ((0, 4, F32), (4, 3, BF16), (7, 1, BF16))


def cube_scatter(keep, give, give_far):
    far = partner(give_far[0])
    near = partner(give)
    relay = partner(along((keep[3] + far).astype(BF16)))
    two = partner(along((keep[2] + near[2]).astype(BF16)))
    three = along((keep[1] + near[1] + relay).astype(BF16))
    return [keep[0], near[0], two, three]


def body(activations, curvature, basis, krylov):
    dp, mp = lax.axis_size("dp"), lax.axis_size("mp")
    tok = activations.shape[0]
    length = krylov.shape[0]
    rows = length // (TILES * LANES)
    cw = curvature.shape[1] // CHUNKS
    d = lax.axis_index("dp")
    m = lax.axis_index("mp").astype(jnp.int32).reshape(1)
    total = float(length * dp * mp)
    scale = 1.0 / (tok * dp)
    cube = dp == 8

    packed = pack(m, krylov.reshape(length // LANES, LANES), mp, rows, cw, CHUNKS)
    idx = cube_order(d) if cube else jnp.arange(dp, dtype=jnp.int32)
    owned = []
    for c in range(CHUNKS):
        own = assemble(m, shift_mp(packed[c]))
        if cube:
            blocks = cube_gather(own)
            parts = matmuls(idx, activations, curvature, blocks, c, CUBE_GROUPS)
            terms = cube_scatter(*parts)
        else:
            gathered = lax.all_gather(own, "dp", axis=0, tiled=False)
            blocks = [gathered[k] for k in range(dp)]
            (part,) = matmuls(idx, activations, curvature, blocks, c, ((0, dp, F32),))
            terms = [lax.psum_scatter(part, "dp", scatter_dimension=0, tiled=False)]
        owned.append(shift_mp(split(m, terms, mp, scale)))

    blocks = 8
    gram_tiles = gram(basis, blocks)
    u, sums = project(m, gram_tiles, basis, owned, mp, dp * mp, blocks)
    sums = lax.all_to_all(sums, ("dp", "mp"), 0, 0, tiled=True)
    out, hess = residual(sums, basis, u, total, blocks)
    return out.reshape(length), hess[0, : basis.shape[0] + 1]


def solution(mesh):
    return jax.shard_map(
        body,
        mesh=mesh,
        in_specs=(P("dp", None), P("dp", "mp"), P(None, ("dp", "mp")), P(("dp", "mp"))),
        out_specs=(P(("dp", "mp")), P()),
        check_vma=False,
    )
```
